128 devices in a mesh: hemi: 2 (over core), blk: 64 (over x, z, y).
Axes of the slice: x: 4, y: 4, z: 4, core: 2. Of those that a mesh axis runs over, the one named last changes fastest.
Arguments:
- data: float32 [2, 256, 256, 2, 256], P('hemi', 'blk'), may hold values from -6 to 6
- signal: float32 [2, 256, 256, 2, 256], P('hemi', 'blk'), may hold values from -6 to 6
- noise: float32 [2, 256], P('hemi', 'blk'), may hold values from 0.5 to 48
- cycle_weight: float32 [256], replicated, may hold values from 2 to 8
- cl: float32 [16384], replicated, may hold values from 0.05 to 20
- legendre: bfloat16 [256, 2, 256, 8192], P('blk', 'hemi'), may hold values from -0.0625 to 0.0625
- m_table: int32 [256], P('blk'), may hold values from 0 to 16383, as said below
Outputs:
- new_signal: float32 [2, 256, 256, 2, 256], P('hemi', 'blk')
The draws below stay inside these ranges and needn't reach their ends.
Inputs may be any that keep to these rules, and one draw needn't show every extreme that they name: `m_table`: the 256 entries are distinct; which slot holds which order is drawn.
All inputs are finite; a program needn't handle non-finite values.
Results may differ from the reference program's by a relative error of at most 0.003.
Values sent between devices are 32-bit elements; how exact they have to be, the bound alone decides.
No kernel may reach another device: no remote copies, remote signals or barrier semaphores. Data moves between devices by JAX's collectives and lax.ppermute only.
A program may use at most 128 MiB of HBM per device.

```python
import math
import jax
import jax.numpy as jnp
from jax import lax

L = 16384
J = 8192
R = 256
M = 256
NS = 256


def draw_m_table(key, part):
    stride = L // M
    offsets = jax.random.randint(jax.random.fold_in(key, 11), (M,), 0, stride)
    offsets = offsets.at[0].set(0).at[M - 1].set(stride - 1)
    values = jnp.arange(M, dtype=jnp.int32) * stride + offsets.astype(jnp.int32)
    order = jax.random.permutation(jax.random.fold_in(key, 12), M)
    return values[order].astype(jnp.int32)


def draw_noise(key, part):
    lowest = jnp.exp(jax.random.uniform(jax.random.fold_in(key, 21), (), jnp.float32, math.log(0.5), math.log(3.0)))
    spread = jnp.exp(jax.random.uniform(jax.random.fold_in(key, 22), (2 * R,), jnp.float32, 0.0, math.log(16.0)))
    planted = jax.random.randint(jax.random.fold_in(key, 23), (), 0, 2 * R)
    spread = jnp.where(jnp.arange(2 * R, dtype=jnp.int32) == planted, jnp.float32(1.0), spread)
    return (lowest * spread).reshape(2, R).astype(jnp.float32)


def level_of(key, dims, pieces, low, largest):
    factor_of, own = 1.0, jax.random.fold_in(key, 6)
    for axis_at, blocks in pieces:
        draws = jnp.exp(jax.random.uniform(jax.random.fold_in(own, axis_at), (blocks,), jnp.float32, low / len(pieces), largest / len(pieces)))
        factor_of = factor_of * jnp.repeat(draws, dims[axis_at] // blocks).reshape([-1 if axis == axis_at else 1 for axis in range(len(dims))])
    return factor_of


def gaussian(rng, shape, width, bound, split=(), kind=jnp.bfloat16):
    loudness = level_of(rng, shape, split, -0.22, 0.18) if split else 1.0
    array = jax.random.normal(rng, shape, jnp.float32) * width * loudness
    return jnp.minimum(jnp.maximum(array, -bound), bound).astype(kind)


def setup_inputs(seed: int = 0) -> dict:
    keys = jax.random.split(jax.random.key(seed), 8)
    data = gaussian(keys[0], (2, R, M, 2, NS), 1.0, 6.0, ((0, 2), (1, 64)), jnp.float32)
    signal = gaussian(keys[1], (2, R, M, 2, NS), 1.0, 6.0, ((0, 2), (1, 64)), jnp.float32)
    noise = draw_noise(jax.random.fold_in(keys[7], 71), 0)
    cycle_weight = jnp.clip(jnp.exp(jax.random.uniform(keys[3], (R,), jnp.float32, math.log(2.0), math.log(8.0))), 2.0, 8.0)
    cl = jnp.clip(jnp.exp(jax.random.uniform(keys[4], (L,), jnp.float32, math.log(0.05), math.log(20.0))), 0.05, 20.0)
    legendre = gaussian(keys[5], (M, 2, R, J), J ** -0.5, 0.0625, ((0, 64), (1, 2)))
    m_table = draw_m_table(jax.random.fold_in(keys[7], 71), 0)
    return {"data": data, "signal": signal, "noise": noise, "cycle_weight": cycle_weight, "cl": cl, "legendre": legendre, "m_table": m_table}


def one_slot(args):
    slot_rows, table, m_value, cycle_weight, cl, tau = args
    first = slot_rows[0]
    second = slot_rows[1]
    outputs = []
    for parity in range(2):
        sign_factor = jnp.float32(1 - 2 * parity)
        weighted = (cycle_weight[:, None, None] * (first + sign_factor * second)).astype(jnp.bfloat16)
        cycle_rows = weighted.reshape(weighted.shape[0], -1)
        coeffs = jnp.dot(cycle_rows.T, table[parity], preferred_element_type=jnp.float32)
        column = jnp.arange(J, dtype=jnp.int32)
        multipole = (m_value + parity + 2 * column).astype(jnp.int32)
        live = multipole < L
        cl_cols = jnp.take(cl, jnp.minimum(multipole, L - 1).astype(jnp.int32))
        gain = jnp.where(live, cl_cols / (cl_cols + tau), jnp.float32(0.0))
        filtered = (coeffs * gain[None, :]).astype(jnp.bfloat16)
        synth = jnp.dot(table[parity], filtered.T, preferred_element_type=jnp.float32)
        outputs.append(synth)
    return jnp.stack(outputs)


def reference(data, signal, noise, cycle_weight, cl, legendre, m_table):
    tau = jnp.min(noise)
    noise_cols = noise[:, :, None, None, None]
    messenger = (tau * data + (noise_cols - tau) * signal) / noise_cols
    per_slot = jnp.transpose(messenger, (2, 0, 1, 3, 4))

    def run(slot_index):
        return one_slot((per_slot[slot_index], legendre[slot_index], m_table[slot_index], cycle_weight, cl, tau))

    synth = lax.map(run, jnp.arange(M, dtype=jnp.int32))
    synth = synth.reshape(M, 2, R, 2, NS)
    synth = jnp.transpose(synth, (1, 2, 0, 3, 4))
    north = synth[0] + synth[1]
    south = synth[0] - synth[1]
    return jnp.stack([north, south])
```

```python
import jax
import jax.numpy as jnp
from jax import lax
from jax.experimental import pallas as pl
from jax.experimental.pallas import tpu as pltpu
from jax.sharding import PartitionSpec as P

ALL = ("blk", "hemi")
BLK = 64
DEV = 128
SLOTS = 4
CYCLES = 256
COLS = 8192
BJ = 1024
NBLK = COLS // BJ
LANES = 128
SWAP = [(0, 1), (1, 0)]


def to_tiles(array):
    array = array.reshape(4, 256, 2, 2, LANES).transpose(0, 1, 3, 2, 4)
    return array.reshape(2, 2, BLK, 2, 8, LANES)


def from_tiles(array):
    return array.reshape(4, 256, 2, 2, LANES).transpose(0, 1, 3, 2, 4).reshape(1, 4, 256, 2, 256)


def messenger_kernel(idx_ref, noise_ref, weight_ref, all_noise_ref, data_ref, signal_ref, data2_ref, signal2_ref, *outs):
    hemi = idx_ref[0]
    blk = idx_ref[1]
    sign = (1 - 2 * hemi).astype(jnp.float32)
    tau = jnp.min(all_noise_ref[...])
    other_row = all_noise_ref[pl.ds(2 * blk + 1 - hemi, 1), :]
    lane = lax.broadcasted_iota(jnp.int32, (1, LANES), 1)
    for r in range(2):
        weight = weight_ref[4 * blk + 2 * hemi + r]
        own_noise = jnp.full((1, LANES), noise_ref[0, 2 * hemi + r], jnp.float32)
        other_noise = jnp.full((1, LANES), jnp.sum(jnp.where(lane == 2 * hemi + r, other_row, 0.0)), jnp.float32)
        coefs = []
        for n in (own_noise, other_noise):
            scale = weight / n
            coefs.append((scale * tau, scale * (n - tau)))
        (a, b), (a2, b2) = coefs
        for kk in range(2):
            own = a * data_ref[r, :, kk] + b * signal_ref[r, :, kk]
            other = a2 * data2_ref[r, :, kk] + b2 * signal2_ref[r, :, kk]
            out, at = (outs[0], kk) if len(outs) == 1 else (outs[kk], 0)
            out[:, 0, r, at] = own + other
            out[:, 1, r, at] = sign * (own - other)


def messenger(idx, noise, weight, all_noise, data, signal, data2, signal2, chunks):
    step = 16
    kk = 2 // chunks
    mine = pl.BlockSpec((None, 2, step, 2, 8, LANES), lambda i, idx: (idx[0], 0, i, 0, 0, 0))
    theirs = pl.BlockSpec((2, step, 2, 8, LANES), lambda i, idx: (0, i, 0, 0, 0))
    out = pl.BlockSpec((step, 2, 2, kk, 8, LANES), lambda i, idx: (i, 0, 0, 0, 0, 0))
    smem = pl.BlockSpec(memory_space=pltpu.SMEM)
    return pl.pallas_call(
        messenger_kernel,
        grid_spec=pltpu.PrefetchScalarGridSpec(
            num_scalar_prefetch=1,
            grid=(BLK // step,),
            in_specs=[smem, smem, pl.BlockSpec((DEV, LANES), lambda i, idx: (0, 0)), mine, mine, theirs, theirs],
            out_specs=[out] * chunks,
        ),
        out_shape=[jax.ShapeDtypeStruct((BLK, 2, 2, kk, 8, LANES), jnp.float32)] * chunks,
        compiler_params=pltpu.CompilerParams(vmem_limit_bytes=16 << 20),
        cost_estimate=pl.CostEstimate(flops=4 << 20, bytes_accessed=6 << 20, transcendentals=0),
        name="messenger",
    )(idx, noise, weight, all_noise, data, signal, data2, signal2)


def filter_kernel(first, count, idx_ref, m_ref, noise_ref, cl_ref, rows_ref, leg_hbm, out_ref, leg, sem, halves, acc, picked, gain):
    hemi = idx_ref[0]
    tau = jnp.min(noise_ref[...])
    stride = 4 * count

    def offset_of(slot):
        return (m_ref[first + slot] + hemi) >> 1

    def blocks_of(slot):
        return (COLS - offset_of(slot) + BJ - 1) // BJ

    def copy(slot, j):
        cols = pl.ds(pl.multiple_of(j * BJ, BJ), BJ)
        return pltpu.make_async_copy(leg_hbm.at[first + slot, :, cols], leg.at[slot, :, cols], sem.at[slot, j])

    for slot in range(count):
        @pl.loop(0, blocks_of(slot))
        def _(j, slot=slot):
            copy(slot, j).start()

    src = lax.broadcasted_iota(jnp.int32, (LANES, LANES), 0)
    dst = lax.broadcasted_iota(jnp.int32, (LANES, LANES), 1)
    pick = jnp.where(src == 2 * (dst & 63) + (dst >> 6), 1.0, 0.0).astype(jnp.float32)
    gain[...] = jnp.dot(cl_ref[...], pick, precision=lax.Precision.HIGHEST, preferred_element_type=jnp.float32)
    low = gain[pl.ds(0, 64, stride=2), :]
    high = gain[pl.ds(1, 64, stride=2), :]
    lane = lax.broadcasted_iota(jnp.int32, (64, LANES), 1)
    picked[...] = jnp.zeros_like(picked)
    picked[0, 0:64, :] = jnp.where(lane < 64, low, pltpu.roll(high, 64, 1))
    picked[1, 0:64, :] = jnp.where(lane < 64, pltpu.roll(low, 64, 1), high)

    @pl.loop(0, count)
    def _(slot):
        start = offset_of(slot)
        parity = (m_ref[first + slot] + hemi) & 1
        row, turn = start >> 7, start & 127
        back = (LANES - turn) & 127
        here = pltpu.roll(picked[parity, pl.ds(row, 64), :], back, 1)
        after = pltpu.roll(picked[parity, pl.ds(row + 1, 64), :], back, 1)
        cl_cols = jnp.where(lane < LANES - turn, here, after)
        gain[0:64, :] = cl_cols / (cl_cols + tau)
        for q in range(4):
            part = rows_ref[pl.ds(slot * 4 + q, CYCLES, stride=stride), :]
            halves[q * LANES:(q + 1) * LANES, :] = part.T.astype(jnp.bfloat16)
        acc[...] = jnp.zeros_like(acc)

        @pl.loop(0, blocks_of(slot))
        def _(j):
            copy(slot, j).wait()
            table = leg[slot, :, pl.ds(pl.multiple_of(j * BJ, BJ), BJ)]
            coeffs = jnp.dot(halves[...], table, preferred_element_type=jnp.float32)
            row_of = [gain[pl.ds(j * (BJ // LANES) + i, 1), :] for i in range(BJ // LANES)]
            filtered = (coeffs * jnp.concatenate(row_of, axis=1)).astype(jnp.bfloat16)
            acc[...] += lax.dot_general(filtered, table, (((1,), (1,)), ((), ())), preferred_element_type=jnp.float32)

        for q in range(4):
            out_ref[pl.ds(slot * 4 + q, CYCLES, stride=stride), :] = acc[q * LANES:(q + 1) * LANES, :].T


def filtering(first, count, idx, m_table, all_noise, cl, rows, legendre):
    smem = pl.BlockSpec(memory_space=pltpu.SMEM)
    vmem = pl.BlockSpec(memory_space=pltpu.VMEM)

    def body(*refs):
        filter_kernel(first, count, *refs)

    return pl.pallas_call(
        body,
        in_specs=[smem, smem, vmem, vmem, vmem, pl.BlockSpec(memory_space=pl.ANY)],
        out_specs=vmem,
        out_shape=jax.ShapeDtypeStruct((CYCLES * 4 * count, LANES), jnp.float32),
        scratch_shapes=[
            pltpu.VMEM((count, CYCLES, COLS), jnp.bfloat16),
            pltpu.SemaphoreType.DMA((count, NBLK)),
            pltpu.VMEM((512, CYCLES), jnp.bfloat16),
            pltpu.VMEM((512, CYCLES), jnp.float32),
            pltpu.VMEM((2, 136, LANES), jnp.float32),
            pltpu.VMEM((LANES, LANES), jnp.float32),
        ],
        compiler_params=pltpu.CompilerParams(vmem_limit_bytes=48 << 20),
        cost_estimate=pl.CostEstimate(flops=count * (4 << 30), bytes_accessed=count * (5 << 20), transcendentals=0),
        name="filtering",
    )(idx, m_table, all_noise, cl, rows, legendre)


def combine_kernel(idx_ref, *refs):
    out, parts = refs[-1], refs[:-1]
    turn = idx_ref[1]
    sign = (turn * (1 - 2 * idx_ref[0])).astype(jnp.float32)
    at = 0
    for part in parts:
        for kk in range(part.shape[3]):
            for r in range(2):
                out[r, :, at] = part[:, 0, r, kk] + sign * part[:, 1, r, kk]
            at += 1


def combine(idx, parts, turn):
    step = 16
    code = jnp.stack([idx[0], jnp.int32(turn)])
    ins = [pl.BlockSpec((step, 2, 2, p.shape[3], 8, LANES), lambda i, idx: (i, 0, 0, 0, 0, 0)) for p in parts]
    if turn > 0:
        out_spec = pl.BlockSpec((None, 2, step, 2, 8, LANES), lambda i, idx: (idx[0], 0, i, 0, 0, 0))
        out_shape = (2, 2, BLK, 2, 8, LANES)
    else:
        out_spec = pl.BlockSpec((2, step, 2, 8, LANES), lambda i, idx: (0, i, 0, 0, 0))
        out_shape = (2, BLK, 2, 8, LANES)
    return pl.pallas_call(
        combine_kernel,
        grid_spec=pltpu.PrefetchScalarGridSpec(num_scalar_prefetch=1, grid=(BLK // step,), in_specs=ins, out_specs=out_spec),
        out_shape=jax.ShapeDtypeStruct(out_shape, jnp.float32),
        compiler_params=pltpu.CompilerParams(vmem_limit_bytes=16 << 20),
        cost_estimate=pl.CostEstimate(flops=1 << 20, bytes_accessed=3 << 20, transcendentals=0),
        name="combine_own" if turn > 0 else "combine_other",
    )(code, *parts)


def place_kernel(idx_ref, part_ref, whole_ref, out_ref):
    out_ref[...] = part_ref[...]


def place(idx, part, whole):
    step = 32
    return pl.pallas_call(
        place_kernel,
        grid_spec=pltpu.PrefetchScalarGridSpec(
            num_scalar_prefetch=1,
            grid=(BLK // step,),
            in_specs=[
                pl.BlockSpec((2, step, 2, 8, LANES), lambda i, idx: (0, i, 0, 0, 0)),
                pl.BlockSpec(memory_space=pl.ANY),
            ],
            out_specs=pl.BlockSpec((None, 2, step, 2, 8, LANES), lambda i, idx: (1 - idx[0], 0, i, 0, 0, 0)),
        ),
        out_shape=jax.ShapeDtypeStruct(whole.shape, jnp.float32),
        input_output_aliases={2: 0},
        compiler_params=pltpu.CompilerParams(vmem_limit_bytes=16 << 20),
        cost_estimate=pl.CostEstimate(flops=0, bytes_accessed=2 << 20, transcendentals=0),
        name="place",
    )(idx, part, whole)


CHUNKS = 1


def shards(data, signal, noise, cycle_weight, cl, legendre, m_table):
    hemi = lax.axis_index("hemi")
    blk = lax.axis_index("blk")
    idx = jnp.stack([hemi, blk]).astype(jnp.int32)
    seen = jnp.broadcast_to(jnp.tile(noise.reshape(4), LANES // 4)[None, None, :], (DEV, 1, LANES))
    all_noise = lax.all_to_all(seen, ALL, 0, 0, tiled=True).reshape(DEV, LANES)
    data, signal = to_tiles(data), to_tiles(signal)
    other = 1 - hemi
    data2 = lax.ppermute(lax.dynamic_index_in_dim(data, other, 0, keepdims=False), "hemi", SWAP)
    signal2 = lax.ppermute(lax.dynamic_index_in_dim(signal, other, 0, keepdims=False), "hemi", SWAP)
    sums = messenger(idx, noise, cycle_weight, all_noise, data, signal, data2, signal2, CHUNKS)
    table = legendre.reshape(SLOTS, CYCLES, COLS)
    cl_rows = cl.reshape(LANES, LANES)
    count = SLOTS // CHUNKS
    synth = []
    for chunk, part in enumerate(sums):
        modes = lax.all_to_all(part.reshape(DEV, 8 * count, LANES), ALL, 0, 0, tiled=True)
        rows = modes.reshape(CYCLES * 4 * count, LANES)
        done = filtering(chunk * count, count, idx, m_table, all_noise, cl_rows, rows, table)
        back = lax.all_to_all(done.reshape(DEV, 8 * count, LANES), ALL, 0, 0, tiled=True)
        synth.append(back.reshape(BLK, 2, 2, count // 2, 8, LANES))
    sent = lax.ppermute(combine(idx, synth, -1), "hemi", SWAP)
    whole = combine(idx, synth, 1)
    return from_tiles(place(idx, sent, whole))


def solution(mesh):
    return jax.shard_map(
        shards,
        mesh=mesh,
        in_specs=(
            P("hemi", "blk", None, None, None),
            P("hemi", "blk", None, None, None),
            P("hemi", "blk"),
            P(),
            P(),
            P("blk", "hemi", None, None),
            P("blk"),
        ),
        out_specs=P("hemi", "blk", None, None, None),
        check_vma=False,
    )
```

```python
import jax
import jax.numpy as jnp
from jax import lax
from jax.experimental import pallas as pl
from jax.experimental.pallas import tpu as pltpu
from jax.sharding import PartitionSpec as P

ALL = ("blk", "hemi")
BLK = 64
DEV = 128
SLOTS = 4
CYCLES = 256
COLS = 8192
UNIT = 512
UNIT_BITS = 9
SIZES = (4096, 2048, 1024, 512)
LANES = 128
SWAP = [(0, 1), (1, 0)]


def to_tiles(array):
    array = array.reshape(4, 256, 2, 2, LANES).transpose(0, 1, 3, 2, 4)
    return array.reshape(2, 2, BLK, 2, 8, LANES)


def from_tiles(array):
    return array.reshape(4, 256, 2, 2, LANES).transpose(0, 1, 3, 2, 4).reshape(1, 4, 256, 2, 256)


BIG = 3e38
VMEM_ALL = 67043328


STAGES = 4


def messenger_kernel(all_noise_ref, weight_hbm, data, signal, data2, signal2, out, ins, sums, weights, in_sem, out_sem, weight_sem):
    hemi = lax.axis_index("hemi")
    blk = lax.axis_index("blk")
    step = BLK // STAGES
    sources = (data, signal, data2, signal2)

    def fetch(n, i):
        at = pl.ds(i * step, step)
        return pltpu.make_async_copy(sources[n].at[hemi, :, at], ins.at[n, :, at], in_sem.at[n, i])

    def store(i):
        at = pl.ds(i * step, step)
        return pltpu.make_async_copy(sums.at[at], out.at[at], out_sem.at[i])

    weight_copy = pltpu.make_async_copy(weight_hbm, weights, weight_sem)
    weight_copy.start()
    for i in range(STAGES):
        for n in range(4):
            fetch(n, i).start()
    sign = (1 - 2 * hemi).astype(jnp.float32)
    tau = jnp.min(all_noise_ref[...])
    lane = lax.broadcasted_iota(jnp.int32, (1, LANES), 1)
    own_row = all_noise_ref[pl.ds(2 * blk + hemi, 1), :]
    other_row = all_noise_ref[pl.ds(2 * blk + 1 - hemi, 1), :]

    def pick(row, at):
        return jnp.sum(jnp.where(lane == at, row, 0.0), axis=1, keepdims=True)

    coefs = []
    first = 4 * blk + 2 * hemi
    weight_copy.wait()
    weight_row = weights[pl.ds(first >> 7, 1), :]
    for r in range(2):
        weight = pick(weight_row, (first & 127) + r)
        for n in (pick(own_row, 2 * hemi + r), pick(other_row, 2 * hemi + r)):
            scale = weight / n
            coefs.append((jnp.broadcast_to(scale * tau, (8, LANES)), jnp.broadcast_to(scale * (n - tau), (8, LANES))))
    small = 4
    for i in range(STAGES):
        for n in range(4):
            fetch(n, i).wait()

        @pl.loop(0, step // small)
        def _(j, i=i):
            at = pl.ds(i * step + j * small, small)
            for r in range(2):
                (a, b), (a2, b2) = coefs[2 * r:2 * r + 2]
                for kk in range(2):
                    own = a * ins[0, r, at, kk] + b * ins[1, r, at, kk]
                    other = a2 * ins[2, r, at, kk] + b2 * ins[3, r, at, kk]
                    sums[at, 0, r, kk] = own + other
                    sums[at, 1, r, kk] = sign * (own - other)

        store(i).start()
    for i in range(STAGES):
        store(i).wait()


def messenger(all_noise, weight, data, signal, data2, signal2):
    hbm = pl.BlockSpec(memory_space=pltpu.HBM)
    return pl.pallas_call(
        messenger_kernel,
        in_specs=[pl.BlockSpec(memory_space=pltpu.VMEM)] + [hbm] * 5,
        out_specs=hbm,
        out_shape=jax.ShapeDtypeStruct((BLK, 2, 2, 2, 8, LANES), jnp.float32),
        scratch_shapes=[
            pltpu.VMEM((4, 2, BLK, 2, 8, LANES), jnp.float32),
            pltpu.VMEM((BLK, 2, 2, 2, 8, LANES), jnp.float32),
            pltpu.VMEM((2, LANES), jnp.float32),
            pltpu.SemaphoreType.DMA((4, STAGES)),
            pltpu.SemaphoreType.DMA((STAGES,)),
            pltpu.SemaphoreType.DMA,
        ],
        compiler_params=pltpu.CompilerParams(vmem_limit_bytes=VMEM_ALL),
        cost_estimate=pl.CostEstimate(flops=4 << 20, bytes_accessed=6 << 20, transcendentals=0),
        name="messenger",
    )(all_noise, weight, data, signal, data2, signal2)


def prepare_kernel(m_ref, cl_ref, out_ref, mixed, picked):
    hemi = lax.axis_index("hemi")
    src = lax.broadcasted_iota(jnp.int32, (LANES, LANES), 0)
    dst = lax.broadcasted_iota(jnp.int32, (LANES, LANES), 1)
    pick = jnp.where(src == 2 * (dst & 63) + (dst >> 6), 1.0, 0.0).astype(jnp.float32)
    mixed[...] = jnp.dot(cl_ref[...], pick, precision=lax.Precision.HIGHEST, preferred_element_type=jnp.float32)
    low = mixed[pl.ds(0, 64, stride=2), :]
    high = mixed[pl.ds(1, 64, stride=2), :]
    lane = lax.broadcasted_iota(jnp.int32, (64, LANES), 1)
    picked[...] = jnp.zeros_like(picked)
    picked[0, 0:64, :] = jnp.where(lane < 64, low, pltpu.roll(high, 64, 1))
    picked[1, 0:64, :] = jnp.where(lane < 64, pltpu.roll(low, 64, 1), high)
    for slot in range(SLOTS):
        start = (m_ref[slot] + hemi) >> 1
        parity = (m_ref[slot] + hemi) & 1
        row, turn = start >> 7, start & 127
        back = (LANES - turn) & 127
        here = pltpu.roll(picked[parity, pl.ds(row, 64), :], back, 1)
        after = pltpu.roll(picked[parity, pl.ds(row + 1, 64), :], back, 1)
        out_ref[slot] = jnp.where(lane < LANES - turn, here, after)


def prepare(m_table, cl):
    smem = pl.BlockSpec(memory_space=pltpu.SMEM)
    vmem = pl.BlockSpec(memory_space=pltpu.VMEM)
    return pl.pallas_call(
        prepare_kernel,
        in_specs=[smem, vmem],
        out_specs=vmem,
        out_shape=jax.ShapeDtypeStruct((SLOTS, 64, LANES), jnp.float32),
        scratch_shapes=[pltpu.VMEM((LANES, LANES), jnp.float32), pltpu.VMEM((2, 136, LANES), jnp.float32)],
        compiler_params=pltpu.CompilerParams(vmem_limit_bytes=4 << 20),
        cost_estimate=pl.CostEstimate(flops=4 << 20, bytes_accessed=1 << 18, transcendentals=0),
        name="prepare",
    )(m_table, cl)


def filter_kernel(m_ref, all_noise_ref, cl_ref, rows_ref, leg_hbm, out_ref, leg, halves, acc, gain, leg_sem):
    hemi = lax.axis_index("hemi")
    stride = 4 * SLOTS

    def units_of(slot):
        return (COLS - ((m_ref[slot] + hemi) >> 1) + UNIT - 1) >> UNIT_BITS

    def fetch(slot, j):
        cols = pl.ds(pl.multiple_of(j * UNIT, UNIT), UNIT)
        return pltpu.make_async_copy(leg_hbm.at[slot, :, cols], leg.at[slot, :, cols], leg_sem.at[slot, j])

    for slot in range(SLOTS):
        @pl.loop(0, units_of(slot))
        def _(j, slot=slot):
            fetch(slot, j).start()

    tau = jnp.min(all_noise_ref[...])

    @pl.loop(0, SLOTS)
    def _(slot):
        for q in range(4):
            part = rows_ref[pl.ds(slot * 4 + q, CYCLES, stride=stride), :]
            halves[slot, q * LANES:(q + 1) * LANES, :] = part.T.astype(jnp.bfloat16)

    def block(slot, at, size):
        @pl.loop(0, size // UNIT)
        def _(i):
            fetch(slot, at + i).wait()

        table = leg[slot, :, pl.ds(pl.multiple_of(at * UNIT, UNIT), size)]
        coeffs = jnp.dot(halves[slot], table, preferred_element_type=jnp.float32)
        row_of = [gain[pl.ds(at * (UNIT // LANES) + i, 1), :] for i in range(size // LANES)]
        filtered = (coeffs * jnp.concatenate(row_of, axis=1)).astype(jnp.bfloat16)
        acc[...] += lax.dot_general(table, filtered, (((1,), (1,)), ((), ())), preferred_element_type=jnp.float32)

    @pl.loop(0, SLOTS)
    def _(slot):
        units = units_of(slot)
        cl_cols = cl_ref[slot]
        gain[...] = cl_cols / (cl_cols + tau)
        acc[...] = jnp.zeros_like(acc)
        per = SIZES[0] // UNIT
        whole = units >> (per.bit_length() - 1)

        @pl.loop(0, whole)
        def _(j):
            block(slot, j * per, SIZES[0])

        at = whole * per
        for size in SIZES[1:]:
            per = size // UNIT

            @pl.when((units & per) != 0)
            def _(at=at, size=size):
                block(slot, at, size)

            at = at + (units & per)
        for q in range(4):
            out_ref[pl.ds(slot * 4 + q, CYCLES, stride=stride), :] = acc[:, q * LANES:(q + 1) * LANES]


def filtering(m_table, all_noise, cl_cols, rows, legendre):
    smem = pl.BlockSpec(memory_space=pltpu.SMEM)
    vmem = pl.BlockSpec(memory_space=pltpu.VMEM)
    hbm = pl.BlockSpec(memory_space=pltpu.HBM)
    return pl.pallas_call(
        filter_kernel,
        in_specs=[smem, vmem, vmem, vmem, hbm],
        out_specs=vmem,
        out_shape=jax.ShapeDtypeStruct((CYCLES * 16, LANES), jnp.float32),
        scratch_shapes=[
            pltpu.VMEM((SLOTS, CYCLES, COLS), jnp.bfloat16),
            pltpu.VMEM((SLOTS, 512, CYCLES), jnp.bfloat16),
            pltpu.VMEM((CYCLES, 512), jnp.float32),
            pltpu.VMEM((64, LANES), jnp.float32),
            pltpu.SemaphoreType.DMA((SLOTS, COLS // UNIT)),
        ],
        compiler_params=pltpu.CompilerParams(vmem_limit_bytes=44 << 20),
        cost_estimate=pl.CostEstimate(flops=16 << 30, bytes_accessed=20 << 20, transcendentals=0),
        name="filtering",
    )(m_table, all_noise, cl_cols, rows, legendre)


def combine_kernel(own, parts, out, *scratch):
    hemi = lax.axis_index("hemi")
    sign = (1 - 2 * hemi).astype(jnp.float32)
    if not own:
        sign = -sign
    target = scratch[0] if own else out
    small = 8

    @pl.loop(0, BLK // small)
    def _(i):
        at = pl.ds(i * small, small)
        for r in range(2):
            for kk in range(2):
                target[r, at, kk] = parts[at, 0, r, kk] + sign * parts[at, 1, r, kk]

    if own:
        copy = pltpu.make_async_copy(scratch[0], out.at[hemi], scratch[1])
        copy.start()
        copy.wait()


def combine(parts, own):
    half = (2, BLK, 2, 8, LANES)
    vmem = pl.BlockSpec(memory_space=pltpu.VMEM)

    def body(*refs):
        combine_kernel(own, *refs)

    return pl.pallas_call(
        body,
        in_specs=[vmem],
        out_specs=pl.BlockSpec(memory_space=pltpu.HBM) if own else vmem,
        out_shape=jax.ShapeDtypeStruct((2,) + half if own else half, jnp.float32),
        scratch_shapes=[pltpu.VMEM(half, jnp.float32), pltpu.SemaphoreType.DMA] if own else [],
        compiler_params=pltpu.CompilerParams(vmem_limit_bytes=6 << 20),
        cost_estimate=pl.CostEstimate(flops=1 << 20, bytes_accessed=3 << 20, transcendentals=0),
        name="combine_own" if own else "combine_other",
    )(parts)


def place_kernel(part_ref, whole_ref, out_ref, sem):
    copy = pltpu.make_async_copy(part_ref, out_ref.at[1 - lax.axis_index("hemi")], sem)
    copy.start()
    copy.wait()


def place(part, whole):
    hbm = pl.BlockSpec(memory_space=pltpu.HBM)
    return pl.pallas_call(
        place_kernel,
        in_specs=[pl.BlockSpec(memory_space=pltpu.VMEM), hbm],
        out_specs=hbm,
        out_shape=jax.ShapeDtypeStruct(whole.shape, jnp.float32),
        scratch_shapes=[pltpu.SemaphoreType.DMA],
        input_output_aliases={1: 0},
        compiler_params=pltpu.CompilerParams(vmem_limit_bytes=4 << 20),
        cost_estimate=pl.CostEstimate(flops=0, bytes_accessed=2 << 20, transcendentals=0),
        name="place",
    )(part, whole)


def shards(data, signal, noise, cycle_weight, cl, legendre, m_table):
    seen = jnp.broadcast_to(jnp.pad(noise, ((0, 0), (0, LANES - 4)), constant_values=BIG)[None], (DEV, 1, LANES))
    all_noise = lax.all_to_all(seen, ALL, 0, 0, tiled=True).reshape(DEV, LANES)
    data, signal = to_tiles(data), to_tiles(signal)
    data2 = lax.ppermute(data, "hemi", SWAP)
    signal2 = lax.ppermute(signal, "hemi", SWAP)
    sums = messenger(all_noise, cycle_weight.reshape(2, LANES), data, signal, data2, signal2)
    cl_cols = prepare(m_table, cl.reshape(LANES, LANES))
    modes = lax.all_to_all(sums.reshape(DEV, 32, LANES), ALL, 0, 0, tiled=True)
    done = filtering(m_table, all_noise, cl_cols, modes.reshape(CYCLES * 16, LANES), legendre.reshape(SLOTS, CYCLES, COLS))
    back = lax.all_to_all(done.reshape(DEV, 32, LANES), ALL, 0, 0, tiled=True)
    parts = back.reshape(BLK, 2, 2, 2, 8, LANES)
    sent = lax.ppermute(combine(parts, False), "hemi", SWAP)
    whole = combine(parts, True)
    return from_tiles(place(sent, whole))


def solution(mesh):
    return jax.shard_map(
        shards,
        mesh=mesh,
        in_specs=(
            P("hemi", "blk", None, None, None),
            P("hemi", "blk", None, None, None),
            P("hemi", "blk"),
            P(),
            P(),
            P("blk", "hemi", None, None),
            P("blk"),
        ),
        out_specs=P("hemi", "blk", None, None, None),
        check_vma=False,
    )
```

```python
import jax
import jax.numpy as jnp
from jax import lax
from jax.experimental import pallas as pl
from jax.experimental.pallas import tpu as pltpu
from jax.sharding import PartitionSpec as P


ALL = ("blk", "hemi")
BLK = 64
DEV = 128
SLOTS = 4
CYCLES = 256
COLS = 8192
UNIT = 1024
UNIT_BITS = 10
LANES = 128
SWAP = [(0, 1), (1, 0)]


def to_tiles(array):
    array = array.reshape(4, 256, 2, 2, LANES).transpose(0, 1, 3, 2, 4)
    return array.reshape(2, 2, BLK, 2, 8, LANES)


def from_tiles(array):
    return array.reshape(4, 256, 2, 2, LANES).transpose(0, 1, 3, 2, 4).reshape(1, 4, 256, 2, 256)


BIG = 3e38
VMEM_ALL = 67043328


STAGES = 4


def messenger_kernel(all_noise_ref, weight_hbm, data, signal, data2, signal2, out, ins, sums, weights, in_sem, out_sem, weight_sem):
    hemi = lax.axis_index("hemi")
    blk = lax.axis_index("blk")
    step = BLK // STAGES
    sources = (data, signal, data2, signal2)

    def fetch(n, i):
        at = pl.ds(i * step, step)
        return pltpu.make_async_copy(sources[n].at[hemi, :, at], ins.at[n, :, at], in_sem.at[n, i])

    def store(i):
        at = pl.ds(i * step, step)
        return pltpu.make_async_copy(sums.at[at], out.at[at], out_sem.at[i])

    weight_copy = pltpu.make_async_copy(weight_hbm, weights, weight_sem)
    weight_copy.start()
    for i in range(STAGES):
        for n in range(4):
            fetch(n, i).start()
    sign = (1 - 2 * hemi).astype(jnp.float32)
    tau = jnp.min(all_noise_ref[...])
    lane = lax.broadcasted_iota(jnp.int32, (1, LANES), 1)
    own_row = all_noise_ref[pl.ds(2 * blk + hemi, 1), :]
    other_row = all_noise_ref[pl.ds(2 * blk + 1 - hemi, 1), :]

    def pick(row, at):
        return jnp.sum(jnp.where(lane == at, row, 0.0), axis=1, keepdims=True)

    coefs = []
    first = 4 * blk + 2 * hemi
    weight_copy.wait()
    weight_row = weights[pl.ds(first >> 7, 1), :]
    for r in range(2):
        weight = pick(weight_row, (first & 127) + r)
        for n in (pick(own_row, 2 * hemi + r), pick(other_row, 2 * hemi + r)):
            scale = weight / n
            coefs.append((jnp.broadcast_to(scale * tau, (8, LANES)), jnp.broadcast_to(scale * (n - tau), (8, LANES))))
    small = 4
    for i in range(STAGES):
        for n in range(4):
            fetch(n, i).wait()

        @pl.loop(0, step // small)
        def _(j, i=i):
            at = pl.ds(i * step + j * small, small)
            for r in range(2):
                (a, b), (a2, b2) = coefs[2 * r:2 * r + 2]
                for kk in range(2):
                    own = a * ins[0, r, at, kk] + b * ins[1, r, at, kk]
                    other = a2 * ins[2, r, at, kk] + b2 * ins[3, r, at, kk]
                    sums[at, 0, r, kk] = own + other
                    sums[at, 1, r, kk] = sign * (own - other)

        store(i).start()
    for i in range(STAGES):
        store(i).wait()


def messenger(all_noise, weight, data, signal, data2, signal2):
    hbm = pl.BlockSpec(memory_space=pltpu.HBM)
    return pl.pallas_call(
        messenger_kernel,
        in_specs=[pl.BlockSpec(memory_space=pltpu.VMEM)] + [hbm] * 5,
        out_specs=hbm,
        out_shape=jax.ShapeDtypeStruct((BLK, 2, 2, 2, 8, LANES), jnp.float32),
        scratch_shapes=[
            pltpu.VMEM((4, 2, BLK, 2, 8, LANES), jnp.float32),
            pltpu.VMEM((BLK, 2, 2, 2, 8, LANES), jnp.float32),
            pltpu.VMEM((2, LANES), jnp.float32),
            pltpu.SemaphoreType.DMA((4, STAGES)),
            pltpu.SemaphoreType.DMA((STAGES,)),
            pltpu.SemaphoreType.DMA,
        ],
        compiler_params=pltpu.CompilerParams(vmem_limit_bytes=VMEM_ALL),
        cost_estimate=pl.CostEstimate(flops=4 << 20, bytes_accessed=6 << 20, transcendentals=0),
        name="messenger",
    )(all_noise, weight, data, signal, data2, signal2)


def gram_kernel(m_ref, all_noise_ref, cl_ref, leg_hbm, out_ref, leg, acc, gain, mixed, picked, leg_sem):
    hemi = lax.axis_index("hemi")

    def units_of(slot):
        return (COLS - ((m_ref[slot] + hemi) >> 1) + UNIT - 1) >> UNIT_BITS

    def fetch(slot, j):
        cols = pl.ds(pl.multiple_of(j * UNIT, UNIT), UNIT)
        return pltpu.make_async_copy(leg_hbm.at[slot, :, cols], leg.at[slot, :, cols], leg_sem.at[slot, j])

    for slot in range(SLOTS):
        @pl.loop(0, units_of(slot))
        def _(j, slot=slot):
            fetch(slot, j).start()

    tau = jnp.min(all_noise_ref[...])
    src = lax.broadcasted_iota(jnp.int32, (LANES, LANES), 0)
    dst = lax.broadcasted_iota(jnp.int32, (LANES, LANES), 1)
    pick = jnp.where(src == 2 * (dst & 63) + (dst >> 6), 1.0, 0.0).astype(jnp.float32)
    mixed[...] = jnp.dot(cl_ref[...], pick, precision=lax.Precision.HIGHEST, preferred_element_type=jnp.float32)
    low = mixed[pl.ds(0, 64, stride=2), :]
    high = mixed[pl.ds(1, 64, stride=2), :]
    lane = lax.broadcasted_iota(jnp.int32, (64, LANES), 1)
    picked[...] = jnp.zeros_like(picked)
    picked[0, 0:64, :] = jnp.where(lane < 64, low, pltpu.roll(high, 64, 1))
    picked[1, 0:64, :] = jnp.where(lane < 64, pltpu.roll(low, 64, 1), high)

    @pl.loop(0, SLOTS)
    def _(slot):
        start = (m_ref[slot] + hemi) >> 1
        parity = (m_ref[slot] + hemi) & 1
        row, turn = start >> 7, start & 127
        back = (LANES - turn) & 127
        here = pltpu.roll(picked[parity, pl.ds(row, 64), :], back, 1)
        after = pltpu.roll(picked[parity, pl.ds(row + 1, 64), :], back, 1)
        cl_cols = jnp.where(lane < LANES - turn, here, after)
        gain[...] = cl_cols / (cl_cols + tau)
        acc[...] = jnp.zeros_like(acc)

        @pl.loop(0, units_of(slot))
        def _(j):
            fetch(slot, j).wait()
            table = leg[slot, :, pl.ds(pl.multiple_of(j * UNIT, UNIT), UNIT)]
            row_of = [gain[pl.ds(j * (UNIT // LANES) + i, 1), :] for i in range(UNIT // LANES)]
            scaled = (table.astype(jnp.float32) * jnp.concatenate(row_of, axis=1)).astype(jnp.bfloat16)
            acc[...] += lax.dot_general(scaled, table, (((1,), (1,)), ((), ())), preferred_element_type=jnp.float32)

        whole = acc[...]
        out_ref[slot, 0] = whole.astype(jnp.bfloat16)
        out_ref[slot, 1] = (whole - out_ref[slot, 0].astype(jnp.float32)).astype(jnp.bfloat16)


def gram(m_table, all_noise, cl, legendre):
    smem = pl.BlockSpec(memory_space=pltpu.SMEM)
    vmem = pl.BlockSpec(memory_space=pltpu.VMEM)
    hbm = pl.BlockSpec(memory_space=pltpu.HBM)
    return pl.pallas_call(
        gram_kernel,
        in_specs=[smem, vmem, vmem, hbm],
        out_specs=vmem,
        out_shape=jax.ShapeDtypeStruct((SLOTS, 2, CYCLES, CYCLES), jnp.bfloat16),
        scratch_shapes=[
            pltpu.VMEM((SLOTS, CYCLES, COLS), jnp.bfloat16),
            pltpu.VMEM((CYCLES, CYCLES), jnp.float32),
            pltpu.VMEM((64, LANES), jnp.float32),
            pltpu.VMEM((LANES, LANES), jnp.float32),
            pltpu.VMEM((2, 136, LANES), jnp.float32),
            pltpu.SemaphoreType.DMA((SLOTS, COLS // UNIT)),
        ],
        compiler_params=pltpu.CompilerParams(vmem_limit_bytes=40 << 20),
        cost_estimate=pl.CostEstimate(flops=4 << 30, bytes_accessed=17 << 20, transcendentals=0),
        name="gram",
    )(m_table, all_noise, cl, legendre)


def apply_kernel(gram_ref, rows_ref, out_ref, halves):
    stride = 4 * SLOTS

    @pl.loop(0, SLOTS)
    def _(slot):
        for q in range(4):
            part = rows_ref[pl.ds(slot * 4 + q, CYCLES, stride=stride), :]
            halves[:, q * LANES:(q + 1) * LANES] = part.astype(jnp.bfloat16)
        synth = jnp.dot(gram_ref[slot, 0], halves[...], preferred_element_type=jnp.float32)
        synth = synth + jnp.dot(gram_ref[slot, 1], halves[...], preferred_element_type=jnp.float32)
        for q in range(4):
            out_ref[pl.ds(slot * 4 + q, CYCLES, stride=stride), :] = synth[:, q * LANES:(q + 1) * LANES]


def apply(grams, rows):
    vmem = pl.BlockSpec(memory_space=pltpu.VMEM)
    return pl.pallas_call(
        apply_kernel,
        in_specs=[vmem, vmem],
        out_specs=vmem,
        out_shape=jax.ShapeDtypeStruct((CYCLES * 16, LANES), jnp.float32),
        scratch_shapes=[pltpu.VMEM((CYCLES, 512), jnp.bfloat16)],
        compiler_params=pltpu.CompilerParams(vmem_limit_bytes=10 << 20),
        cost_estimate=pl.CostEstimate(flops=1 << 29, bytes_accessed=5 << 20, transcendentals=0),
        name="apply",
    )(grams, rows)


def combine_kernel(own, parts, out, *scratch):
    hemi = lax.axis_index("hemi")
    sign = (1 - 2 * hemi).astype(jnp.float32)
    if not own:
        sign = -sign
    target = scratch[0] if own else out
    small = 8

    @pl.loop(0, BLK // small)
    def _(i):
        at = pl.ds(i * small, small)
        for r in range(2):
            for kk in range(2):
                target[r, at, kk] = parts[at, 0, r, kk] + sign * parts[at, 1, r, kk]

    if own:
        copy = pltpu.make_async_copy(scratch[0], out.at[hemi], scratch[1])
        copy.start()
        copy.wait()


def combine(parts, own):
    half = (2, BLK, 2, 8, LANES)
    vmem = pl.BlockSpec(memory_space=pltpu.VMEM)

    def body(*refs):
        combine_kernel(own, *refs)

    return pl.pallas_call(
        body,
        in_specs=[vmem],
        out_specs=pl.BlockSpec(memory_space=pltpu.HBM) if own else vmem,
        out_shape=jax.ShapeDtypeStruct((2,) + half if own else half, jnp.float32),
        scratch_shapes=[pltpu.VMEM(half, jnp.float32), pltpu.SemaphoreType.DMA] if own else [],
        compiler_params=pltpu.CompilerParams(vmem_limit_bytes=6 << 20),
        cost_estimate=pl.CostEstimate(flops=1 << 20, bytes_accessed=3 << 20, transcendentals=0),
        name="combine_own" if own else "combine_other",
    )(parts)


def place_kernel(part_ref, whole_ref, out_ref, sem):
    copy = pltpu.make_async_copy(part_ref, out_ref.at[1 - lax.axis_index("hemi")], sem)
    copy.start()
    copy.wait()


def place(part, whole):
    hbm = pl.BlockSpec(memory_space=pltpu.HBM)
    return pl.pallas_call(
        place_kernel,
        in_specs=[pl.BlockSpec(memory_space=pltpu.VMEM), hbm],
        out_specs=hbm,
        out_shape=jax.ShapeDtypeStruct(whole.shape, jnp.float32),
        scratch_shapes=[pltpu.SemaphoreType.DMA],
        input_output_aliases={1: 0},
        compiler_params=pltpu.CompilerParams(vmem_limit_bytes=4 << 20),
        cost_estimate=pl.CostEstimate(flops=0, bytes_accessed=2 << 20, transcendentals=0),
        name="place",
    )(part, whole)


def shards(data, signal, noise, cycle_weight, cl, legendre, m_table):
    seen = jnp.broadcast_to(jnp.pad(noise, ((0, 0), (0, LANES - 4)), constant_values=BIG)[None], (DEV, 1, LANES))
    all_noise = lax.all_to_all(seen, ALL, 0, 0, tiled=True).reshape(DEV, LANES)
    data, signal = to_tiles(data), to_tiles(signal)
    data2 = lax.ppermute(data, "hemi", SWAP)
    signal2 = lax.ppermute(signal, "hemi", SWAP)
    sums = messenger(all_noise, cycle_weight.reshape(2, LANES), data, signal, data2, signal2)
    grams = gram(m_table, all_noise, cl.reshape(LANES, LANES), legendre.reshape(SLOTS, CYCLES, COLS))
    modes = lax.all_to_all(sums.reshape(DEV, 32, LANES), ALL, 0, 0, tiled=True)
    done = apply(grams, modes.reshape(CYCLES * 16, LANES))
    back = lax.all_to_all(done.reshape(DEV, 32, LANES), ALL, 0, 0, tiled=True)
    parts = back.reshape(BLK, 2, 2, 2, 8, LANES)
    sent = lax.ppermute(combine(parts, False), "hemi", SWAP)
    whole = combine(parts, True)
    return from_tiles(place(sent, whole))


def solution(mesh):
    return jax.shard_map(
        shards,
        mesh=mesh,
        in_specs=(
            P("hemi", "blk", None, None, None),
            P("hemi", "blk", None, None, None),
            P("hemi", "blk"),
            P(),
            P(),
            P("blk", "hemi", None, None),
            P("blk"),
        ),
        out_specs=P("hemi", "blk", None, None, None),
        check_vma=False,
    )
```

```python
import jax
import jax.numpy as jnp
from jax import lax
from jax.experimental import pallas as pl
from jax.experimental.pallas import tpu as pltpu
from jax.sharding import PartitionSpec as P


ALL = ("hemi", "blk")
BLK = 64
DEV = 128
SLOTS = 4
CYCLES = 256
COLS = 8192
UNIT = 1024
UNIT_BITS = 10
LANES = 128
SWAP = [(0, 1), (1, 0)]


def to_tiles(array):
    array = array.reshape(4, 256, 2, 2, LANES).transpose(0, 1, 3, 2, 4)
    return array.reshape(4, BLK, 2, 8, LANES)


def from_tiles(array):
    return array.reshape(4, 256, 2, 2, LANES).transpose(0, 1, 3, 2, 4).reshape(1, 4, 256, 2, 256)


BIG = 3e38
VMEM_ALL = 67043328


STAGES = 8


def messenger_kernel(all_noise_ref, weight_hbm, data, signal, out, ins, sums, weights, in_sem, out_sem, weight_sem):
    blk = lax.axis_index("blk")
    me = lax.axis_index("hemi") * BLK + blk
    step = BLK // STAGES
    sources = (data, signal)

    def fetch(n, i):
        at = pl.ds(i * step, step)
        return pltpu.make_async_copy(sources[n].at[:, at], ins.at[n, :, at], in_sem.at[n, i])

    def store(i):
        at = pl.ds(i * step, step)
        return pltpu.make_async_copy(sums.at[:, at], out.at[:, at], out_sem.at[i])

    weight_copy = pltpu.make_async_copy(weight_hbm, weights, weight_sem)
    weight_copy.start()
    for i in range(STAGES):
        for n in range(2):
            fetch(n, i).start()
    tau = jnp.min(all_noise_ref[...])
    lane = lax.broadcasted_iota(jnp.int32, (1, LANES), 1)
    own_row = all_noise_ref[pl.ds(me, 1), :]

    def pick(row, at):
        return jnp.sum(jnp.where(lane == at, row, 0.0), axis=1, keepdims=True)

    coefs = []
    weight_copy.wait()
    weight_row = weights[pl.ds((4 * blk) >> 7, 1), :]
    for r in range(4):
        n = pick(own_row, r)
        scale = pick(weight_row, ((4 * blk) & 127) + r) / n
        coefs.append((jnp.broadcast_to(scale * tau, (8, LANES)), jnp.broadcast_to(scale * (n - tau), (8, LANES))))
    small = 4
    for i in range(STAGES):
        for n in range(2):
            fetch(n, i).wait()

        @pl.loop(0, step // small)
        def _(j, i=i):
            at = pl.ds(i * step + j * small, small)
            for r in range(4):
                a, b = coefs[r]
                for pair in range(2):
                    sums[pair, at, r] = a * ins[0, r, at, pair] + b * ins[1, r, at, pair]

        store(i).start()
    for i in range(STAGES):
        store(i).wait()


def messenger(all_noise, weight, data, signal):
    hbm = pl.BlockSpec(memory_space=pltpu.HBM)
    return pl.pallas_call(
        messenger_kernel,
        in_specs=[pl.BlockSpec(memory_space=pltpu.VMEM)] + [hbm] * 3,
        out_specs=hbm,
        out_shape=jax.ShapeDtypeStruct((2, BLK, 4, 8, LANES), jnp.float32),
        scratch_shapes=[
            pltpu.VMEM((2, 4, BLK, 2, 8, LANES), jnp.float32),
            pltpu.VMEM((2, BLK, 4, 8, LANES), jnp.float32),
            pltpu.VMEM((2, LANES), jnp.float32),
            pltpu.SemaphoreType.DMA((2, STAGES)),
            pltpu.SemaphoreType.DMA((STAGES,)),
            pltpu.SemaphoreType.DMA,
        ],
        compiler_params=pltpu.CompilerParams(vmem_limit_bytes=VMEM_ALL),
        cost_estimate=pl.CostEstimate(flops=4 << 20, bytes_accessed=6 << 20, transcendentals=0),
        name="messenger",
    )(all_noise, weight, data, signal)


def gram_kernel(m_ref, all_noise_ref, cl_ref, leg_hbm, out_ref, leg, acc, gain, mixed, picked, leg_sem):
    hemi = lax.axis_index("hemi")

    def units_of(slot):
        return (COLS - ((m_ref[slot] + hemi) >> 1) + UNIT - 1) >> UNIT_BITS

    def fetch(slot, j):
        cols = pl.ds(pl.multiple_of(j * UNIT, UNIT), UNIT)
        return pltpu.make_async_copy(leg_hbm.at[slot, :, cols], leg.at[slot, :, cols], leg_sem.at[slot, j])

    for slot in range(SLOTS):
        @pl.loop(0, units_of(slot))
        def _(j, slot=slot):
            fetch(slot, j).start()

    tau = jnp.min(all_noise_ref[...])
    src = lax.broadcasted_iota(jnp.int32, (LANES, LANES), 0)
    dst = lax.broadcasted_iota(jnp.int32, (LANES, LANES), 1)
    pick = jnp.where(src == 2 * (dst & 63) + (dst >> 6), 1.0, 0.0).astype(jnp.float32)
    mixed[...] = jnp.dot(cl_ref[...], pick, precision=lax.Precision.HIGHEST, preferred_element_type=jnp.float32)
    low = mixed[pl.ds(0, 64, stride=2), :]
    high = mixed[pl.ds(1, 64, stride=2), :]
    lane = lax.broadcasted_iota(jnp.int32, (64, LANES), 1)
    picked[...] = jnp.zeros_like(picked)
    picked[0, 0:64, :] = jnp.where(lane < 64, low, pltpu.roll(high, 64, 1))
    picked[1, 0:64, :] = jnp.where(lane < 64, pltpu.roll(low, 64, 1), high)

    @pl.loop(0, SLOTS)
    def _(slot):
        start = (m_ref[slot] + hemi) >> 1
        parity = (m_ref[slot] + hemi) & 1
        row, turn = start >> 7, start & 127
        back = (LANES - turn) & 127
        here = pltpu.roll(picked[parity, pl.ds(row, 64), :], back, 1)
        after = pltpu.roll(picked[parity, pl.ds(row + 1, 64), :], back, 1)
        cl_cols = jnp.where(lane < LANES - turn, here, after)
        gain[...] = cl_cols / (cl_cols + tau)
        acc[...] = jnp.zeros_like(acc)

        @pl.loop(0, units_of(slot))
        def _(j):
            fetch(slot, j).wait()
            table = leg[slot, :, pl.ds(pl.multiple_of(j * UNIT, UNIT), UNIT)]
            row_of = [gain[pl.ds(j * (UNIT // LANES) + i, 1), :] for i in range(UNIT // LANES)]
            scaled = (table.astype(jnp.float32) * jnp.concatenate(row_of, axis=1)).astype(jnp.bfloat16)
            acc[...] += lax.dot_general(scaled, table, (((1,), (1,)), ((), ())), preferred_element_type=jnp.float32)

        out_ref[slot >> 1, slot & 1] = acc[...]


def gram(m_table, all_noise, cl, legendre):
    smem = pl.BlockSpec(memory_space=pltpu.SMEM)
    vmem = pl.BlockSpec(memory_space=pltpu.VMEM)
    hbm = pl.BlockSpec(memory_space=pltpu.HBM)
    return pl.pallas_call(
        gram_kernel,
        in_specs=[smem, vmem, vmem, hbm],
        out_specs=vmem,
        out_shape=jax.ShapeDtypeStruct((2, 2, CYCLES, CYCLES), jnp.float32),
        scratch_shapes=[
            pltpu.VMEM((SLOTS, CYCLES, COLS), jnp.bfloat16),
            pltpu.VMEM((CYCLES, CYCLES), jnp.float32),
            pltpu.VMEM((64, LANES), jnp.float32),
            pltpu.VMEM((LANES, LANES), jnp.float32),
            pltpu.VMEM((2, 136, LANES), jnp.float32),
            pltpu.SemaphoreType.DMA((SLOTS, COLS // UNIT)),
        ],
        compiler_params=pltpu.CompilerParams(vmem_limit_bytes=40 << 20),
        cost_estimate=pl.CostEstimate(flops=4 << 30, bytes_accessed=17 << 20, transcendentals=0),
        name="gram",
    )(m_table, all_noise, cl, legendre)


def arrange_kernel(own_ref, other_ref, out_ref):
    hemi = lax.axis_index("hemi")
    for slot in range(2):
        for parity in range(2):
            whole = jnp.where(hemi == parity, own_ref[hemi, slot], other_ref[hemi, slot])
            near = whole.astype(jnp.bfloat16)
            out_ref[slot, parity, 0] = near
            out_ref[slot, parity, 1] = (whole - near.astype(jnp.float32)).astype(jnp.bfloat16)


def arrange(own, other):
    vmem = pl.BlockSpec(memory_space=pltpu.VMEM)
    return pl.pallas_call(
        arrange_kernel,
        in_specs=[vmem, vmem],
        out_specs=vmem,
        out_shape=jax.ShapeDtypeStruct((2, 2, 2, CYCLES, CYCLES), jnp.bfloat16),
        compiler_params=pltpu.CompilerParams(vmem_limit_bytes=8 << 20),
        cost_estimate=pl.CostEstimate(flops=1 << 20, bytes_accessed=3 << 20, transcendentals=0),
        name="arrange",
    )(own, other)


def apply_kernel(matrix_ref, rows_ref, out_ref, halves):
    south = CYCLES * 8
    for slot in range(2):
        for q in range(4):
            at = slot * 4 + q
            first = rows_ref[pl.ds(at, CYCLES, stride=8), :]
            second = rows_ref[pl.ds(south + at, CYCLES, stride=8), :]
            halves[slot, 0, :, q * LANES:(q + 1) * LANES] = (first + second).astype(jnp.bfloat16)
            halves[slot, 1, :, q * LANES:(q + 1) * LANES] = (first - second).astype(jnp.bfloat16)
    for slot in range(2):
        synth = []
        for parity in range(2):
            synth.append(
                jnp.dot(matrix_ref[slot, parity, 0], halves[slot, parity], preferred_element_type=jnp.float32)
                + jnp.dot(matrix_ref[slot, parity, 1], halves[slot, parity], preferred_element_type=jnp.float32)
            )
        for q in range(4):
            at = slot * 4 + q
            even, odd = synth[0][:, q * LANES:(q + 1) * LANES], synth[1][:, q * LANES:(q + 1) * LANES]
            out_ref[pl.ds(at, CYCLES, stride=8), :] = even + odd
            out_ref[pl.ds(south + at, CYCLES, stride=8), :] = even - odd


def apply(matrices, rows):
    vmem = pl.BlockSpec(memory_space=pltpu.VMEM)
    return pl.pallas_call(
        apply_kernel,
        in_specs=[vmem, vmem],
        out_specs=vmem,
        out_shape=jax.ShapeDtypeStruct((CYCLES * 16, LANES), jnp.float32),
        scratch_shapes=[pltpu.VMEM((2, 2, CYCLES, 512), jnp.bfloat16)],
        compiler_params=pltpu.CompilerParams(vmem_limit_bytes=12 << 20),
        cost_estimate=pl.CostEstimate(flops=1 << 29, bytes_accessed=6 << 20, transcendentals=0),
        name="apply",
    )(matrices, rows)


def place_kernel(parts, out, sem):
    copies = [
        pltpu.make_async_copy(parts.at[pair, :, r], out.at[r, :, pair], sem.at[pair, r]) for pair in range(2) for r in range(4)
    ]
    for copy in copies:
        copy.start()
    for copy in copies:
        copy.wait()


def place(parts):
    return pl.pallas_call(
        place_kernel,
        in_specs=[pl.BlockSpec(memory_space=pltpu.VMEM)],
        out_specs=pl.BlockSpec(memory_space=pltpu.HBM),
        out_shape=jax.ShapeDtypeStruct((4, BLK, 2, 8, LANES), jnp.float32),
        scratch_shapes=[pltpu.SemaphoreType.DMA((2, 4))],
        compiler_params=pltpu.CompilerParams(vmem_limit_bytes=4 << 20),
        cost_estimate=pl.CostEstimate(flops=0, bytes_accessed=4 << 20, transcendentals=0),
        name="place",
    )(parts)


def shards(data, signal, noise, cycle_weight, cl, legendre, m_table):
    seen = jnp.broadcast_to(jnp.pad(noise, ((0, 0), (0, LANES - 4)), constant_values=BIG)[None], (DEV, 1, LANES))
    all_noise = lax.all_to_all(seen, ALL, 0, 0, tiled=True).reshape(DEV, LANES)
    sums = messenger(all_noise, cycle_weight.reshape(2, LANES), to_tiles(data), to_tiles(signal))
    own = gram(m_table, all_noise, cl.reshape(LANES, LANES), legendre.reshape(SLOTS, CYCLES, COLS))
    modes = lax.all_to_all(sums.reshape(DEV, 32, LANES), ALL, 0, 0, tiled=True)
    other = lax.ppermute(own, "hemi", SWAP)
    matrices = arrange(own, other)
    done = apply(matrices, modes.reshape(CYCLES * 16, LANES))
    back = lax.all_to_all(done.reshape(DEV, 32, LANES), ALL, 0, 0, tiled=True)
    return from_tiles(place(back.reshape(2, BLK, 4, 8, LANES)))


def solution(mesh):
    return jax.shard_map(
        shards,
        mesh=mesh,
        in_specs=(
            P("hemi", "blk", None, None, None),
            P("hemi", "blk", None, None, None),
            P("hemi", "blk"),
            P(),
            P(),
            P("blk", "hemi", None, None),
            P("blk"),
        ),
        out_specs=P("hemi", "blk", None, None, None),
        check_vma=False,
    )
```

```python
import jax
import jax.numpy as jnp
from jax import lax
from jax.experimental import pallas as pl
from jax.experimental.pallas import tpu as pltpu
from jax.sharding import PartitionSpec as P


ALL = ("hemi", "blk")
BLK = 64
DEV = 128
SLOTS = 4
CYCLES = 256
COLS = 8192
UNIT = 1024
UNIT_BITS = 10
LANES = 128
SWAP = [(0, 1), (1, 0)]


def to_tiles(array):
    array = array.reshape(4, 256, 2, 2, LANES).transpose(0, 1, 3, 2, 4)
    return array.reshape(4, BLK, 2, 8, LANES)


def from_tiles(array):
    return array.reshape(4, 256, 2, 2, LANES).transpose(0, 1, 3, 2, 4).reshape(1, 4, 256, 2, 256)


BIG = 3e38
VMEM_ALL = 67043328


STAGES = 4


def messenger_kernel(noise_hbm, weight_hbm, data, signal, out, ins, sums, weights, all_noise, in_sem, out_sem, small_sem):
    blk = lax.axis_index("blk")
    me = lax.axis_index("hemi") * BLK + blk
    step = BLK // STAGES
    sources = (data, signal)

    def fetch(n, i):
        at = pl.ds(i * step, step)
        return pltpu.make_async_copy(sources[n].at[:, at], ins.at[n, :, at], in_sem.at[n, i])

    def store(i):
        at = pl.ds(i * step, step)
        return pltpu.make_async_copy(sums.at[:, at], out.at[:, at], out_sem.at[i])

    noise_copy = pltpu.make_async_copy(noise_hbm, all_noise, small_sem.at[0])
    weight_copy = pltpu.make_async_copy(weight_hbm, weights, small_sem.at[1])
    noise_copy.start()
    weight_copy.start()
    for i in range(STAGES):
        for n in range(2):
            fetch(n, i).start()
    lane = lax.broadcasted_iota(jnp.int32, (1, LANES), 1)
    noise_copy.wait()
    tau = jnp.min(all_noise[...])
    own_row = all_noise[pl.ds(me, 1), :]

    def pick(row, at):
        return jnp.sum(jnp.where(lane == at, row, 0.0), axis=1, keepdims=True)

    coefs = []
    weight_copy.wait()
    weight_row = weights[pl.ds((4 * blk) >> 7, 1), :]
    for r in range(4):
        n = pick(own_row, r)
        scale = pick(weight_row, ((4 * blk) & 127) + r) / n
        coefs.append((jnp.broadcast_to(scale * tau, (8, LANES)), jnp.broadcast_to(scale * (n - tau), (8, LANES))))
    small = 4
    for i in range(STAGES):
        for n in range(2):
            fetch(n, i).wait()

        @pl.loop(0, step // small)
        def _(j, i=i):
            at = pl.ds(i * step + j * small, small)
            for r in range(4):
                a, b = coefs[r]
                for pair in range(2):
                    sums[pair, at, r] = a * ins[0, r, at, pair] + b * ins[1, r, at, pair]

        store(i).start()
    for i in range(STAGES):
        store(i).wait()


def messenger(all_noise, weight, data, signal):
    hbm = pl.BlockSpec(memory_space=pltpu.HBM)
    return pl.pallas_call(
        messenger_kernel,
        in_specs=[hbm] * 4,
        out_specs=hbm,
        out_shape=jax.ShapeDtypeStruct((2, BLK, 4, 8, LANES), jnp.float32),
        scratch_shapes=[
            pltpu.VMEM((2, 4, BLK, 2, 8, LANES), jnp.float32),
            pltpu.VMEM((2, BLK, 4, 8, LANES), jnp.float32),
            pltpu.VMEM((2, LANES), jnp.float32),
            pltpu.VMEM((DEV, LANES), jnp.float32),
            pltpu.SemaphoreType.DMA((2, STAGES)),
            pltpu.SemaphoreType.DMA((STAGES,)),
            pltpu.SemaphoreType.DMA((2,)),
        ],
        compiler_params=pltpu.CompilerParams(vmem_limit_bytes=VMEM_ALL),
        cost_estimate=pl.CostEstimate(flops=4 << 20, bytes_accessed=6 << 20, transcendentals=0),
        name="messenger",
    )(all_noise, weight, data, signal)


def gram_kernel(m_ref, all_noise_ref, cl_ref, leg_hbm, out_ref, leg, acc, gain, mixed, picked, leg_sem):
    hemi = lax.axis_index("hemi")

    def units_of(slot):
        return (COLS - ((m_ref[slot] + hemi) >> 1) + UNIT - 1) >> UNIT_BITS

    def fetch(slot, j):
        cols = pl.ds(pl.multiple_of(j * UNIT, UNIT), UNIT)
        return pltpu.make_async_copy(leg_hbm.at[slot, :, cols], leg.at[slot, :, cols], leg_sem.at[slot, j])

    for slot in range(SLOTS):
        @pl.loop(0, units_of(slot))
        def _(j, slot=slot):
            fetch(slot, j).start()

    tau = jnp.min(all_noise_ref[...])
    src = lax.broadcasted_iota(jnp.int32, (LANES, LANES), 0)
    dst = lax.broadcasted_iota(jnp.int32, (LANES, LANES), 1)
    pick = jnp.where(src == 2 * (dst & 63) + (dst >> 6), 1.0, 0.0).astype(jnp.float32)
    mixed[...] = jnp.dot(cl_ref[...], pick, precision=lax.Precision.HIGHEST, preferred_element_type=jnp.float32)
    low = mixed[pl.ds(0, 64, stride=2), :]
    high = mixed[pl.ds(1, 64, stride=2), :]
    lane = lax.broadcasted_iota(jnp.int32, (64, LANES), 1)
    picked[...] = jnp.zeros_like(picked)
    picked[0, 0:64, :] = jnp.where(lane < 64, low, pltpu.roll(high, 64, 1))
    picked[1, 0:64, :] = jnp.where(lane < 64, pltpu.roll(low, 64, 1), high)

    @pl.loop(0, SLOTS)
    def _(slot):
        start = (m_ref[slot] + hemi) >> 1
        parity = (m_ref[slot] + hemi) & 1
        row, turn = start >> 7, start & 127
        back = (LANES - turn) & 127
        here = pltpu.roll(picked[parity, pl.ds(row, 64), :], back, 1)
        after = pltpu.roll(picked[parity, pl.ds(row + 1, 64), :], back, 1)
        cl_cols = jnp.where(lane < LANES - turn, here, after)
        gain[...] = cl_cols / (cl_cols + tau)
        acc[...] = jnp.zeros_like(acc)

        @pl.loop(0, units_of(slot))
        def _(j):
            fetch(slot, j).wait()
            table = leg[slot, :, pl.ds(pl.multiple_of(j * UNIT, UNIT), UNIT)]
            row_of = [gain[pl.ds(j * (UNIT // LANES) + i, 1), :] for i in range(UNIT // LANES)]
            scaled = (table.astype(jnp.float32) * jnp.concatenate(row_of, axis=1)).astype(jnp.bfloat16)
            acc[...] += lax.dot_general(scaled, table, (((1,), (1,)), ((), ())), preferred_element_type=jnp.float32)

        out_ref[slot >> 1, slot & 1] = acc[...]


def gram(m_table, all_noise, cl, legendre):
    smem = pl.BlockSpec(memory_space=pltpu.SMEM)
    vmem = pl.BlockSpec(memory_space=pltpu.VMEM)
    hbm = pl.BlockSpec(memory_space=pltpu.HBM)
    return pl.pallas_call(
        gram_kernel,
        in_specs=[smem, vmem, vmem, hbm],
        out_specs=vmem,
        out_shape=jax.ShapeDtypeStruct((2, 2, CYCLES, CYCLES), jnp.float32),
        scratch_shapes=[
            pltpu.VMEM((SLOTS, CYCLES, COLS), jnp.bfloat16),
            pltpu.VMEM((CYCLES, CYCLES), jnp.float32),
            pltpu.VMEM((64, LANES), jnp.float32),
            pltpu.VMEM((LANES, LANES), jnp.float32),
            pltpu.VMEM((2, 136, LANES), jnp.float32),
            pltpu.SemaphoreType.DMA((SLOTS, COLS // UNIT)),
        ],
        compiler_params=pltpu.CompilerParams(vmem_limit_bytes=40 << 20),
        cost_estimate=pl.CostEstimate(flops=4 << 30, bytes_accessed=17 << 20, transcendentals=0),
        name="gram",
    )(m_table, all_noise, cl, legendre)


def arrange_kernel(own_ref, other_ref, out_ref):
    hemi = lax.axis_index("hemi")
    for slot in range(2):
        for parity in range(2):
            whole = jnp.where(hemi == parity, own_ref[hemi, slot], other_ref[hemi, slot])
            near = whole.astype(jnp.bfloat16)
            out_ref[slot, parity, 0] = near
            out_ref[slot, parity, 1] = (whole - near.astype(jnp.float32)).astype(jnp.bfloat16)


def arrange(own, other):
    vmem = pl.BlockSpec(memory_space=pltpu.VMEM)
    return pl.pallas_call(
        arrange_kernel,
        in_specs=[vmem, vmem],
        out_specs=vmem,
        out_shape=jax.ShapeDtypeStruct((2, 2, 2, CYCLES, CYCLES), jnp.bfloat16),
        compiler_params=pltpu.CompilerParams(vmem_limit_bytes=8 << 20),
        cost_estimate=pl.CostEstimate(flops=1 << 20, bytes_accessed=3 << 20, transcendentals=0),
        name="arrange",
    )(own, other)


def apply_kernel(matrix_ref, rows_ref, out_ref, halves):
    south = CYCLES * 8
    for slot in range(2):
        for q in range(4):
            at = slot * 4 + q
            first = rows_ref[pl.ds(at, CYCLES, stride=8), :]
            second = rows_ref[pl.ds(south + at, CYCLES, stride=8), :]
            halves[slot, 0, :, q * LANES:(q + 1) * LANES] = (first + second).astype(jnp.bfloat16)
            halves[slot, 1, :, q * LANES:(q + 1) * LANES] = (first - second).astype(jnp.bfloat16)
    for slot in range(2):
        synth = []
        for parity in range(2):
            synth.append(
                jnp.dot(matrix_ref[slot, parity, 0], halves[slot, parity], preferred_element_type=jnp.float32)
                + jnp.dot(matrix_ref[slot, parity, 1], halves[slot, parity], preferred_element_type=jnp.float32)
            )
        for q in range(4):
            at = slot * 4 + q
            even, odd = synth[0][:, q * LANES:(q + 1) * LANES], synth[1][:, q * LANES:(q + 1) * LANES]
            out_ref[pl.ds(at, CYCLES, stride=8), :] = even + odd
            out_ref[pl.ds(south + at, CYCLES, stride=8), :] = even - odd


def apply(matrices, rows):
    vmem = pl.BlockSpec(memory_space=pltpu.VMEM)
    return pl.pallas_call(
        apply_kernel,
        in_specs=[vmem, vmem],
        out_specs=vmem,
        out_shape=jax.ShapeDtypeStruct((CYCLES * 16, LANES), jnp.float32),
        scratch_shapes=[pltpu.VMEM((2, 2, CYCLES, 512), jnp.bfloat16)],
        compiler_params=pltpu.CompilerParams(vmem_limit_bytes=12 << 20),
        cost_estimate=pl.CostEstimate(flops=1 << 29, bytes_accessed=6 << 20, transcendentals=0),
        name="apply",
    )(matrices, rows)


def place_kernel(parts, out, sem):
    copies = [
        pltpu.make_async_copy(parts.at[pair, :, r], out.at[r, :, pair], sem.at[pair, r]) for pair in range(2) for r in range(4)
    ]
    for copy in copies:
        copy.start()
    for copy in copies:
        copy.wait()


def place(parts):
    return pl.pallas_call(
        place_kernel,
        in_specs=[pl.BlockSpec(memory_space=pltpu.VMEM)],
        out_specs=pl.BlockSpec(memory_space=pltpu.HBM),
        out_shape=jax.ShapeDtypeStruct((4, BLK, 2, 8, LANES), jnp.float32),
        scratch_shapes=[pltpu.SemaphoreType.DMA((2, 4))],
        compiler_params=pltpu.CompilerParams(vmem_limit_bytes=4 << 20),
        cost_estimate=pl.CostEstimate(flops=0, bytes_accessed=4 << 20, transcendentals=0),
        name="place",
    )(parts)


def shards(data, signal, noise, cycle_weight, cl, legendre, m_table):
    seen = jnp.broadcast_to(jnp.pad(noise, ((0, 0), (0, LANES - 4)), constant_values=BIG)[None], (DEV, 1, LANES))
    all_noise = lax.all_to_all(seen, ALL, 0, 0, tiled=True).reshape(DEV, LANES)
    sums = messenger(all_noise, cycle_weight.reshape(2, LANES), to_tiles(data), to_tiles(signal))
    own = gram(m_table, all_noise, cl.reshape(LANES, LANES), legendre.reshape(SLOTS, CYCLES, COLS))
    modes = lax.all_to_all(sums.reshape(DEV, 32, LANES), ALL, 0, 0, tiled=True)
    other = lax.ppermute(own, "hemi", SWAP)
    matrices = arrange(own, other)
    done = apply(matrices, modes.reshape(CYCLES * 16, LANES))
    back = lax.all_to_all(done.reshape(DEV, 32, LANES), ALL, 0, 0, tiled=True)
    return from_tiles(place(back.reshape(2, BLK, 4, 8, LANES)))


def solution(mesh):
    return jax.shard_map(
        shards,
        mesh=mesh,
        in_specs=(
            P("hemi", "blk", None, None, None),
            P("hemi", "blk", None, None, None),
            P("hemi", "blk"),
            P(),
            P(),
            P("blk", "hemi", None, None),
            P("blk"),
        ),
        out_specs=P("hemi", "blk", None, None, None),
        check_vma=False,
    )
```
